32 devices in a mesh: row: 8 (over z, x), col: 4 (over y, core).
Axes of the slice: x: 2, y: 2, z: 4, core: 2. Of those that a mesh axis runs over, the one named last changes fastest.
Arguments:
- features: float32 [136, 8192], P(None, 'row'), may hold values from -6 to 6
- factor: float32 [8192, 16384], P('row', 'col'), as said below
Outputs:
- panel: float32 [8192, 512], P(('row', 'col'))
The draws below stay inside these ranges and needn't reach their ends.
Inputs may be any that keep to these rules, and one draw needn't show every extreme that they name: `factor`: entries below 18 / sqrt(16384) in magnitude, and the first 512 rows of `reduced` are positive definite.
All inputs are finite; a program needn't handle non-finite values.
Results may differ from the reference program's by a relative error of at most 0.000067.
Values sent between devices are 32-bit elements; how exact they have to be, the bound alone decides.
No kernel may reach another device: no remote copies, remote signals or barrier semaphores. Data moves between devices by JAX's collectives and lax.ppermute only.
A program may use at most 128 MiB of HBM per device.

```python
import math
import jax
import jax.numpy as jnp
from jax import lax

FEAT = 136
B = 512
R = 8192
F = 16384


def draw_factor(key, part):
    entry_scale = 3.0 / math.sqrt(F)
    entries = jnp.clip(jax.random.normal(key, (R, F), jnp.float32), -6.0, 6.0)
    return entries * entry_scale


def steps_of(rng, extent, shards, least, top_value):
    def one(dim, parts):
        draws = jax.random.uniform(jax.random.fold_in(jax.random.fold_in(rng, 6), dim), (parts,), jnp.float32, least / len(shards), top_value / len(shards))
        return jnp.repeat(jnp.exp(draws), extent[dim] // parts).reshape((-1,) + (1,) * (len(extent) - dim - 1))

    level = one(*shards[0])
    for cut in shards[1:]:
        level = level * one(*cut)
    return level


def scatter_about(key, extent, width, limit, pieces=(), kind=jnp.bfloat16):
    values = jax.random.normal(key, extent, jnp.float32) * width
    if len(pieces) > 0:
        values = steps_of(key, extent, pieces, -0.22, 0.18) * values
    return jnp.clip(values, min=-limit, max=limit).astype(kind)


def setup_inputs(seed: int = 0) -> dict:
    arg_keys = jax.random.split(jax.random.key(seed), 3)
    return {
        "features": scatter_about(arg_keys[0], (FEAT, R), 1.0, 6.0, ((1, 8),), jnp.float32),
        "factor": draw_factor(jax.random.fold_in(arg_keys[2], 71), 0),
    }


ridge_value = 40.0

def kernel(points, anchors):
    feature_count = points.shape[0]
    products = lax.dot_general(points.astype(jnp.float32), anchors.astype(jnp.float32), (((0,), (0,)), ((), ())), precision=lax.Precision.HIGHEST, preferred_element_type=jnp.float32)
    norm_points = jnp.sum(points * points, axis=0)
    norm_anchors = jnp.sum(anchors * anchors, axis=0)
    distance = norm_points[:, None] + norm_anchors[None, :] - 2.0 * products
    return products / feature_count + jnp.exp(-distance / (2.0 * feature_count))

def reference(features, factor):
    kernel_panel = kernel(features, features[:, :B])
    update = lax.dot_general(factor.astype(jnp.float32), factor[:B].astype(jnp.float32), (((1,), (1,)), ((), ())), precision=lax.Precision.HIGHEST, preferred_element_type=jnp.float32)
    identity = (jnp.arange(R, dtype=jnp.int32)[:, None] == jnp.arange(B, dtype=jnp.int32)[None, :]).astype(jnp.float32)
    reduced = kernel_panel + ridge_value * identity - update
    lower = jnp.linalg.cholesky(reduced[:B])
    solved = jax.scipy.linalg.solve_triangular(lower, reduced.T, lower=True)
    return solved.T
```

```python
import jax
import jax.numpy as jnp
from jax import lax
from jax.sharding import PartitionSpec as P


B = 512
ridge_value = 40.0
HALVES = 2
DEPTH_CHUNKS = 4
GRAM_SLOT = 2


def exact(a, b, dims):
    return lax.dot_general(
        a, b, (dims, ((), ())), precision=lax.Precision.HIGHEST, preferred_element_type=jnp.float32
    )


def times_rows(block, rows):
    return lax.dot_general(
        block,
        rows,
        (((1,), (1,)), ((), ())),
        precision=lax.Precision.HIGH,
        preferred_element_type=jnp.float32,
    )


def kernel(points, anchors):
    feature_count = points.shape[1]
    products = exact(points, anchors, ((1,), (1,)))
    norm_points = jnp.sum(points * points, axis=1)
    norm_anchors = jnp.sum(anchors * anchors, axis=1)
    distance = norm_points[:, None] + norm_anchors[None, :] - 2.0 * products
    return products / feature_count + jnp.exp(-distance / (2.0 * feature_count))


def swapped(x, bit, count):
    return lax.ppermute(x, "col", [(i, i ^ bit) for i in range(count)])


def reduce_rows(x):
    count = lax.axis_size("col")
    index = lax.axis_index("col")
    x = x.reshape(count, x.shape[0] // count, x.shape[1])
    bit = 1
    while bit < count:
        pairs = x.reshape(x.shape[0] // 2, 2, *x.shape[1:])
        upper = (index & bit) != 0
        kept = jnp.where(upper, pairs[:, 1], pairs[:, 0])
        sent = jnp.where(upper, pairs[:, 0], pairs[:, 1])
        got = swapped(sent, bit, count)
        x = kept + got
        bit *= 2
    return x[0]


def gather_rows(x):
    count = lax.axis_size("col")
    index = lax.axis_index("col")
    x = x[None]
    bit = count // 2
    while bit >= 1:
        got = swapped(x, bit, count)
        upper = (index & bit) != 0
        x = jnp.stack([jnp.where(upper, got, x), jnp.where(upper, x, got)], axis=1)
        x = x.reshape(x.shape[0] * 2, *x.shape[2:])
        bit //= 2
    return x.reshape(x.shape[0] * x.shape[1], x.shape[2])


def ladder(rows):
    length = rows // 2
    along = [(0, 2 * (length - 1))]
    along += [(2 * z, 2 * (z - 1)) for z in range(length - 1, 1, -1)]
    along += [(2 * z + 1, 2 * z + 3) for z in range(length - 1)]
    along += [(2 * length - 1, 1)]
    across = [(0, 1)]
    across += [(2 * z + x, 2 * z + 1 - x) for z in range(1, length) for x in (0, 1)]
    return along, across


def on_device(features, factor):
    rows_dev, depth = factor.shape
    row_count = lax.axis_size("row")
    col_count = lax.axis_size("col")
    col_index = lax.axis_index("col")
    row_index = lax.axis_index("row")
    slab_rows = rows_dev // col_count
    length = row_count // 2
    z, x = row_index // 2, row_index % 2
    is_source = row_index == 0
    along, across = ladder(row_count)
    chunks = HALVES * DEPTH_CHUNKS
    wide, deep = B // HALVES, depth // DEPTH_CHUNKS

    own = factor[:B]
    pieces = []
    for u in range(chunks):
        half, part = divmod(u, DEPTH_CHUNKS)
        pieces.append(own[half * wide : (half + 1) * wide, part * deep : (part + 1) * deep])
    a_own = [p[:, : deep // 2] for p in pieces]
    b_own = [p[:, deep // 2 :] for p in pieces]

    gram = times_rows(own, own)
    gram = reduce_rows(gram)
    share = B // col_count
    points_share = lax.dynamic_slice_in_dim(features, col_index * share, share, 1).T
    feature_count = points_share.shape[1]
    extra = jnp.concatenate(
        [gram, jnp.pad(points_share, ((0, 0), (0, B // 2 - feature_count)))], axis=1
    )
    flat = jnp.pad(extra, ((0, 0), (0, wide * deep // 2 // share - extra.shape[1])))
    spare_shape = flat.shape
    spare = flat.reshape(share * (spare_shape[1] // (deep // 2)), deep // 2)
    b_own.insert(GRAM_SLOT, spare)

    def staged(t, spare, factor):
        slots = list(range(chunks))
        slots.insert(GRAM_SLOT, None)
        pair = []
        for u, part in ((min(t, chunks - 1), 0), (slots[min(t, chunks)], 1)):
            if u is None:
                pair.append(spare)
                continue
            half, k = divmod(u, DEPTH_CHUNKS)
            at = k * deep + part * (deep // 2)
            p = factor[half * wide : (half + 1) * wide, at : at + deep // 2]
            pair.append(jnp.where(is_source, p, jnp.zeros_like(p)))
        return lax.optimization_barrier(tuple(pair))

    along_got, across_got = [], []
    relays_across = (x == 1) & ((z == 0) | (z == length - 1))

    def pick(options, default):
        for condition, value in options:
            default = jnp.where(condition, value, default)
        return default

    def chunk_a(u):
        options = [((x == 0) & (z == k), across_got[u + k + 1]) for k in range(1, length - 1)]
        options += [((x == 1) & (z == k), along_got[u + k]) for k in range(1, length)]
        options += [((x == 1) & (z == 0), across_got[u]), (is_source, a_own[u])]
        return pick(options, across_got[u + length])

    def chunk_b(u):
        options = [((x == 0) & (z == k), along_got[u + length - 1 - k]) for k in range(1, length - 1)]
        options += [((x == 1) & (z == k), across_got[u + length - k]) for k in range(1, length)]
        options += [((x == 1) & (z == 0), along_got[u + 2]), (is_source, b_own[u])]
        return pick(options, along_got[u])

    sums = [None] * HALVES
    reduced_sums = [None] * HALVES

    def update(u, factor):
        half, part = divmod(u, DEPTH_CHUNKS)
        chunk = [chunk_a(u), chunk_b(u if u < GRAM_SLOT else u + 1)]
        chunk = lax.optimization_barrier(jnp.concatenate(chunk, axis=1))
        product = times_rows(factor[:, part * deep : (part + 1) * deep], chunk)
        sums[half] = lax.optimization_barrier(product if part == 0 else sums[half] + product)
        if part == DEPTH_CHUNKS - 1:
            reduced_sums[half] = reduce_rows(sums[half])

    staged_next = staged(0, spare, factor)
    for t in range(chunks + length):
        next_a, next_b = staged_next
        if t == 0:
            send_along, send_across = next_b, next_a
        else:
            send_along = jnp.where(relays_across, across_got[-1], along_got[-1])
            send_across = along_got[-1]
            if t <= chunks:
                send_along = jnp.where(is_source, next_b, send_along)
            if t < chunks:
                send_across = jnp.where(is_source, next_a, send_across)
        send_along, send_across, spare, factor, along_got, across_got = lax.optimization_barrier(
            (send_along, send_across, spare, factor, along_got, across_got)
        )
        if t < chunks:
            staged_next = staged(t + 1, spare, factor)
        u = t - length - 1
        if u >= 0:
            update(u, factor)
        if t < chunks + length - 1:
            got_along = lax.ppermute(send_along, "row", along)
        got_across = lax.ppermute(send_across, "row", across)
        along_got = [*along_got, got_along]
        across_got = [*across_got, got_across]

        slot = t - (length - 1)
        if slot == GRAM_SLOT:
            extra = chunk_b(slot).reshape(spare_shape)[:, : B + B // 2]
            everything = gather_rows(extra)
            gram_all = everything[:, :B]
            panel_points = everything[:, B : B + feature_count]
            pivot_kernel = kernel(panel_points, panel_points)
            pivot = pivot_kernel + ridge_value * jnp.eye(B, dtype=jnp.float32) - gram_all
            lower = jnp.linalg.cholesky(pivot)
            inverse = jax.scipy.linalg.solve_triangular(
                lower, jnp.eye(B, dtype=jnp.float32), lower=True
            )
            own_points = lax.dynamic_slice_in_dim(
                features, col_index * slab_rows, slab_rows, 1
            ).T
            global_rows = (
                row_index * rows_dev + col_index * slab_rows + lax.iota(jnp.int32, slab_rows)
            )
            diagonal = global_rows[:, None] == lax.iota(jnp.int32, B)[None, :]
            slab = kernel(own_points, panel_points) + ridge_value * diagonal.astype(jnp.float32)
    update(chunks - 1, factor)

    result = None
    for half in range(HALVES):
        columns = slice(half * wide, (half + 1) * wide)
        part = exact(slab[:, columns] - reduced_sums[half], inverse[:, columns], ((1,), (1,)))
        result = part if result is None else result + part
    return result


def solution(mesh):
    placed = (P(None, "row"), P("row", "col"))
    return jax.shard_map(
        on_device, mesh=mesh, in_specs=placed, out_specs=P(("row", "col"), None), check_vma=False
    )
```

```python
import functools

import jax
import jax.numpy as jnp
from jax import lax
from jax.experimental import pallas as pl
from jax.experimental.pallas import tpu as pltpu
from jax.sharding import PartitionSpec as P


B = 512
ridge_value = 40.0
HALVES = 2
DEPTH_CHUNKS = 4
GRAM_SLOT = 2

BLOCK = 64
FACTOR_CALLS = ((0,), (1, 2), (3, 4), (5, 6), (7,))


def exact(a, b, dims):
    return lax.dot_general(
        a, b, (dims, ((), ())), precision=lax.Precision.HIGHEST, preferred_element_type=jnp.float32
    )


def times_rows(block, rows):
    return lax.dot_general(
        block,
        rows,
        (((1,), (1,)), ((), ())),
        precision=lax.Precision.HIGH,
        preferred_element_type=jnp.float32,
    )


def kernel(points, anchors):
    feature_count = points.shape[1]
    products = exact(points, anchors, ((1,), (1,)))
    norm_points = jnp.sum(points * points, axis=1)
    norm_anchors = jnp.sum(anchors * anchors, axis=1)
    distance = norm_points[:, None] + norm_anchors[None, :] - 2.0 * products
    return products / feature_count + jnp.exp(-distance / (2.0 * feature_count))


def invert_factor(work):
    groups = work.shape[0] // 8
    width = work.shape[1]
    sublane = lax.broadcasted_iota(jnp.int32, (8, width), 0)

    def lane(v, j):
        return jnp.broadcast_to(v[:, j : j + 1], (8, width))

    def row(v, j):
        return jnp.broadcast_to(v[j : j + 1, :], (8, width))

    def turned(v):
        return pltpu.roll(v, width - 8, 1)

    def group(g, carry):
        at = pl.multiple_of(g * 8, 8)
        top = work[pl.ds(at, 8), :]
        below = [work[8 * i : 8 * i + 8, :] for i in range(groups)]
        corner = [lane(top, j) for j in range(8)]
        pivots = [row(top, j) for j in range(8)]
        columns = [[lane(v, j) for j in range(8)] for v in below[1:]]
        done = top
        for j in range(8):
            p = row(corner[j], j)
            scale = lax.rsqrt(p)
            scale = scale * (1.5 - 0.5 * p * scale * scale)
            factor = corner[j] * scale
            pivots[j] = pivots[j] * scale
            for c in columns:
                c[j] = c[j] * scale
            for m in range(j + 1, 8):
                entry = row(factor, m)
                corner[m] = corner[m] - factor * entry
                pivots[m] = pivots[m] - entry * pivots[j]
                for c in columns:
                    c[m] = c[m] - c[j] * entry
            done = jnp.where(sublane == j, pivots[j], done)
        work[0:8, :] = turned(below[0])
        for i in range(1, groups):
            left = below[i]
            for j in range(8):
                left = left - columns[i - 1][j] * pivots[j]
            work[8 * i : 8 * i + 8, :] = turned(jnp.where(i > g, left, below[i]))
        work[pl.ds(at, 8), :] = turned(done)
        return carry

    lax.fori_loop(0, groups, group, 0)


def factor_body(pieces, given, out, work):
    size = out.shape[0]
    out[...] = given[...]
    identity = (
        lax.broadcasted_iota(jnp.int32, (BLOCK, BLOCK), 0)
        == lax.broadcasted_iota(jnp.int32, (BLOCK, BLOCK), 1)
    ).astype(jnp.float32)
    for p in pieces:
        low, high = p * BLOCK, (p + 1) * BLOCK
        tile = low // 128 * 128
        diagonal = out[low:high, tile : tile + 128][:, low - tile : low - tile + BLOCK]
        work[...] = jnp.concatenate([diagonal, identity], axis=1)
        invert_factor(work)
        rows = exact(work[:, :BLOCK], out[low:high, :], ((1,), (0,)))
        out[low:high, :] = rows
        if high < size:
            tile = high // 128 * 128
            change = exact(rows[:, tile:size], rows, ((0,), (0,)))
            out[high:, :] = out[high:, :] - change[high - tile :, :]


def factored(pieces, state):
    flops = 14 * len(pieces) * BLOCK * state.size
    return pl.pallas_call(
        functools.partial(factor_body, pieces),
        out_shape=jax.ShapeDtypeStruct(state.shape, state.dtype),
        in_specs=[pl.BlockSpec(memory_space=pltpu.VMEM)],
        out_specs=pl.BlockSpec(memory_space=pltpu.VMEM),
        scratch_shapes=[pltpu.VMEM((BLOCK, 2 * BLOCK), jnp.float32)],
        cost_estimate=pl.CostEstimate(
            flops=flops, bytes_accessed=8 * state.size, transcendentals=0
        ),
    )(state)


def swapped(x, bit, count):
    return lax.ppermute(x, "col", [(i, i ^ bit) for i in range(count)])


def reduce_rows(x):
    count = lax.axis_size("col")
    index = lax.axis_index("col")
    x = x.reshape(count, x.shape[0] // count, x.shape[1])
    bit = 1
    while bit < count:
        pairs = x.reshape(x.shape[0] // 2, 2, *x.shape[1:])
        upper = (index & bit) != 0
        kept = jnp.where(upper, pairs[:, 1], pairs[:, 0])
        sent = jnp.where(upper, pairs[:, 0], pairs[:, 1])
        got = swapped(sent, bit, count)
        x = kept + got
        bit *= 2
    return x[0]


def gather_rows(x):
    count = lax.axis_size("col")
    index = lax.axis_index("col")
    x = x[None]
    bit = count // 2
    while bit >= 1:
        got = swapped(x, bit, count)
        upper = (index & bit) != 0
        x = jnp.stack([jnp.where(upper, got, x), jnp.where(upper, x, got)], axis=1)
        x = x.reshape(x.shape[0] * 2, *x.shape[2:])
        bit //= 2
    return x.reshape(x.shape[0] * x.shape[1], x.shape[2])


def ladder(rows):
    length = rows // 2
    along = [(0, 2 * (length - 1))]
    along += [(2 * z, 2 * (z - 1)) for z in range(length - 1, 1, -1)]
    along += [(2 * z + 1, 2 * z + 3) for z in range(length - 1)]
    along += [(2 * length - 1, 1)]
    across = [(0, 1)]
    across += [(2 * z + x, 2 * z + 1 - x) for z in range(1, length) for x in (0, 1)]
    return along, across


def on_device(features, factor):
    rows_dev, depth = factor.shape
    row_count = lax.axis_size("row")
    col_count = lax.axis_size("col")
    col_index = lax.axis_index("col")
    row_index = lax.axis_index("row")
    slab_rows = rows_dev // col_count
    length = row_count // 2
    z, x = row_index // 2, row_index % 2
    is_source = row_index == 0
    along, across = ladder(row_count)
    chunks = HALVES * DEPTH_CHUNKS
    wide, deep = B // HALVES, depth // DEPTH_CHUNKS

    own = factor[:B]
    pieces = []
    for u in range(chunks):
        half, part = divmod(u, DEPTH_CHUNKS)
        pieces.append(own[half * wide : (half + 1) * wide, part * deep : (part + 1) * deep])
    a_own = [p[:, : deep // 2] for p in pieces]
    b_own = [p[:, deep // 2 :] for p in pieces]

    gram = times_rows(own, own)
    gram = reduce_rows(gram)
    share = B // col_count
    points_share = lax.dynamic_slice_in_dim(features, col_index * share, share, 1).T
    feature_count = points_share.shape[1]
    extra = jnp.concatenate(
        [gram, jnp.pad(points_share, ((0, 0), (0, B // 2 - feature_count)))], axis=1
    )
    flat = jnp.pad(extra, ((0, 0), (0, wide * deep // 2 // share - extra.shape[1])))
    spare_shape = flat.shape
    spare = flat.reshape(share * (spare_shape[1] // (deep // 2)), deep // 2)
    b_own.insert(GRAM_SLOT, spare)

    def staged(t, spare, factor):
        slots = list(range(chunks))
        slots.insert(GRAM_SLOT, None)
        pair = []
        for u, part in ((min(t, chunks - 1), 0), (slots[min(t, chunks)], 1)):
            if u is None:
                pair.append(spare)
                continue
            half, k = divmod(u, DEPTH_CHUNKS)
            at = k * deep + part * (deep // 2)
            p = factor[half * wide : (half + 1) * wide, at : at + deep // 2]
            pair.append(jnp.where(is_source, p, jnp.zeros_like(p)))
        return lax.optimization_barrier(tuple(pair))

    along_got, across_got = [], []
    relays_across = (x == 1) & ((z == 0) | (z == length - 1))

    def pick(options, default):
        for condition, value in options:
            default = jnp.where(condition, value, default)
        return default

    def chunk_a(u):
        options = [((x == 0) & (z == k), across_got[u + k + 1]) for k in range(1, length - 1)]
        options += [((x == 1) & (z == k), along_got[u + k]) for k in range(1, length)]
        options += [((x == 1) & (z == 0), across_got[u]), (is_source, a_own[u])]
        return pick(options, across_got[u + length])

    def chunk_b(u):
        options = [((x == 0) & (z == k), along_got[u + length - 1 - k]) for k in range(1, length - 1)]
        options += [((x == 1) & (z == k), across_got[u + length - k]) for k in range(1, length)]
        options += [((x == 1) & (z == 0), along_got[u + 2]), (is_source, b_own[u])]
        return pick(options, along_got[u])

    sums = [None] * HALVES
    reduced_sums = [None] * HALVES

    def update(u, factor):
        half, part = divmod(u, DEPTH_CHUNKS)
        chunk = [chunk_a(u), chunk_b(u if u < GRAM_SLOT else u + 1)]
        chunk = lax.optimization_barrier(jnp.concatenate(chunk, axis=1))
        product = times_rows(factor[:, part * deep : (part + 1) * deep], chunk)
        sums[half] = lax.optimization_barrier(product if part == 0 else sums[half] + product)
        if part == DEPTH_CHUNKS - 1:
            reduced_sums[half] = reduce_rows(sums[half])

    staged_next = staged(0, spare, factor)
    for t in range(chunks + length):
        next_a, next_b = staged_next
        if t == 0:
            send_along, send_across = next_b, next_a
        else:
            send_along = jnp.where(relays_across, across_got[-1], along_got[-1])
            send_across = along_got[-1]
            if t <= chunks:
                send_along = jnp.where(is_source, next_b, send_along)
            if t < chunks:
                send_across = jnp.where(is_source, next_a, send_across)
        send_along, send_across, factor, along_got, across_got = lax.optimization_barrier(
            (send_along, send_across, factor, along_got, across_got)
        )
        if t < chunks:
            staged_next = staged(t + 1, spare, factor)
        u = t - length - 1
        if u >= 0:
            update(u, factor)
        if t < chunks + length - 1:
            got_along = lax.ppermute(send_along, "row", along)
        got_across = lax.ppermute(send_across, "row", across)
        along_got = [*along_got, got_along]
        across_got = [*across_got, got_across]

        slot = t - (length - 1)
        if slot == GRAM_SLOT:
            extra = chunk_b(slot).reshape(spare_shape)[:, : B + B // 2]
            everything = gather_rows(extra)
            gram_all = everything[:, :B]
            panel_points = everything[:, B : B + feature_count]
            pivot_kernel = kernel(panel_points, panel_points)
            pivot = pivot_kernel + ridge_value * jnp.eye(B, dtype=jnp.float32) - gram_all
            state = jnp.concatenate([pivot, jnp.eye(B, dtype=jnp.float32)], axis=1)
            for called in FACTOR_CALLS:
                state = factored(called, state)
            inverse = state[:, B:]
            own_points = lax.dynamic_slice_in_dim(
                features, col_index * slab_rows, slab_rows, 1
            ).T
            global_rows = (
                row_index * rows_dev + col_index * slab_rows + lax.iota(jnp.int32, slab_rows)
            )
            diagonal = global_rows[:, None] == lax.iota(jnp.int32, B)[None, :]
            slab = kernel(own_points, panel_points) + ridge_value * diagonal.astype(jnp.float32)
    update(chunks - 1, factor)

    result = None
    for half in range(HALVES):
        columns = slice(half * wide, (half + 1) * wide)
        part = exact(slab[:, columns] - reduced_sums[half], inverse[:, columns], ((1,), (1,)))
        result = part if result is None else result + part
    return result


def solution(mesh):
    placed = (P(None, "row"), P("row", "col"))
    return jax.shard_map(
        on_device, mesh=mesh, in_specs=placed, out_specs=P(("row", "col"), None), check_vma=False
    )
```

```python
import functools

import jax
import jax.numpy as jnp
from jax import lax
from jax.experimental import pallas as pl
from jax.experimental.pallas import tpu as pltpu
from jax.sharding import PartitionSpec as P


B = 512
ridge_value = 40.0
HALVES = 2
DEPTH_CHUNKS = 4
INVERSE_SLOT = 7

BLOCK = 64
FACTOR_CALLS = ((0, 1), (2, 3), (4, 5), (6,), (7,))
ROW_TILE = 256


def exact(a, b, dims):
    return lax.dot_general(
        a, b, (dims, ((), ())), precision=lax.Precision.HIGHEST, preferred_element_type=jnp.float32
    )


def times_rows(block, rows):
    return lax.dot_general(
        block,
        rows,
        (((1,), (1,)), ((), ())),
        precision=lax.Precision.HIGH,
        preferred_element_type=jnp.float32,
    )


def kernel(points, anchors):
    feature_count = points.shape[1]
    products = exact(points, anchors, ((1,), (1,)))
    norm_points = jnp.sum(points * points, axis=1)
    norm_anchors = jnp.sum(anchors * anchors, axis=1)
    distance = norm_points[:, None] + norm_anchors[None, :] - 2.0 * products
    return products / feature_count + jnp.exp(-distance / (2.0 * feature_count))


def invert_factor(work):
    groups = work.shape[0] // 8
    width = work.shape[1]
    sublane = lax.broadcasted_iota(jnp.int32, (8, width), 0)

    def lane(v, j):
        return jnp.broadcast_to(v[:, j : j + 1], (8, width))

    def row(v, j):
        return jnp.broadcast_to(v[j : j + 1, :], (8, width))

    def turned(v):
        return pltpu.roll(v, width - 8, 1)

    def group(g, carry):
        at = pl.multiple_of(g * 8, 8)
        top = work[pl.ds(at, 8), :]
        below = [work[8 * i : 8 * i + 8, :] for i in range(groups)]
        corner = [lane(top, j) for j in range(8)]
        pivots = [row(top, j) for j in range(8)]
        columns = [[lane(v, j) for j in range(8)] for v in below[1:]]
        done = top
        for j in range(8):
            p = row(corner[j], j)
            scale = lax.rsqrt(p)
            scale = scale * (1.5 - 0.5 * p * scale * scale)
            factor = corner[j] * scale
            pivots[j] = pivots[j] * scale
            for c in columns:
                c[j] = c[j] * scale
            for m in range(j + 1, 8):
                entry = row(factor, m)
                corner[m] = corner[m] - factor * entry
                pivots[m] = pivots[m] - entry * pivots[j]
                for c in columns:
                    c[m] = c[m] - c[j] * entry
            done = jnp.where(sublane == j, pivots[j], done)
        work[0:8, :] = turned(below[0])
        for i in range(1, groups):
            left = below[i]
            for j in range(8):
                left = left - columns[i - 1][j] * pivots[j]
            work[8 * i : 8 * i + 8, :] = turned(jnp.where(i > g, left, below[i]))
        work[pl.ds(at, 8), :] = turned(done)
        return carry

    lax.fori_loop(0, groups, group, 0)


def factor_body(pieces, given, out, work):
    size = out.shape[0]
    out[...] = given[...]
    identity = (
        lax.broadcasted_iota(jnp.int32, (BLOCK, BLOCK), 0)
        == lax.broadcasted_iota(jnp.int32, (BLOCK, BLOCK), 1)
    ).astype(jnp.float32)
    for p in pieces:
        low, high = p * BLOCK, (p + 1) * BLOCK
        tile = low // 128 * 128
        diagonal = out[low:high, tile : tile + 128][:, low - tile : low - tile + BLOCK]
        work[...] = jnp.concatenate([diagonal, identity], axis=1)
        invert_factor(work)
        rows = exact(work[:, :BLOCK], out[low:high, :], ((1,), (0,)))
        out[low:high, :] = rows
        if high < size:
            tile = high // 128 * 128
            change = exact(rows[:, tile:size], rows, ((0,), (0,)))
            out[high:, :] = out[high:, :] - change[high - tile :, :]


def factored(pieces, state):
    flops = 14 * len(pieces) * BLOCK * state.size
    return pl.pallas_call(
        functools.partial(factor_body, pieces),
        out_shape=jax.ShapeDtypeStruct(state.shape, state.dtype),
        in_specs=[pl.BlockSpec(memory_space=pltpu.VMEM)],
        out_specs=pl.BlockSpec(memory_space=pltpu.VMEM),
        scratch_shapes=[pltpu.VMEM((BLOCK, 2 * BLOCK), jnp.float32)],
        cost_estimate=pl.CostEstimate(
            flops=flops, bytes_accessed=8 * state.size, transcendentals=0
        ),
    )(state)


def halves(x):
    high = x.astype(jnp.bfloat16)
    return high, (x - high.astype(jnp.float32)).astype(jnp.bfloat16)


def update_body(sources, own_a, own_b, has_sum, *refs):
    count = 1 + max(i for pair in sources if pair for i in pair)
    row, factor, block, *rest = refs
    got, rest = rest[:count], rest[count:]
    given, rest = (rest[0], rest[1:]) if has_sum else (None, rest)
    out, piece_a, piece_b, high, low, sems = rest
    deep = piece_a.shape[1]

    @pl.when(pl.program_id(0) == 0)
    def _():
        for r, pair in enumerate(sources):

            @pl.when(row[0] == r)
            def _(pair=pair):
                if pair is None:
                    from_a, from_b = factor.at[own_a], factor.at[own_b]
                else:
                    from_a, from_b = got[pair[0]], got[pair[1]]
                copy_a = pltpu.make_async_copy(from_a, piece_a, sems.at[0])
                copy_b = pltpu.make_async_copy(from_b, piece_b, sems.at[1])
                copy_a.start()
                copy_b.start()
                copy_a.wait()
                copy_b.wait()

        high[:, :deep], low[:, :deep] = halves(piece_a[...])
        high[:, deep:], low[:, deep:] = halves(piece_b[...])

    def product(a, b):
        return lax.dot_general(
            a, b[...], (((1,), (1,)), ((), ())), preferred_element_type=jnp.float32
        )

    block_high, block_low = halves(block[...])
    total = product(block_high, high) + (product(block_high, low) + product(block_low, high))
    out[...] = given[...] + total if has_sum else total


def updated(row, factor, part, sources, arrays, own_a, own_b, given):
    rows = factor.shape[0]
    wide, deep = arrays[0].shape
    tile = min(ROW_TILE, rows)
    sum_spec = pl.BlockSpec((tile, wide), lambda i: (i, 0))
    any_spec = pl.BlockSpec(memory_space=pl.ANY)
    in_specs = [
        pl.BlockSpec(memory_space=pltpu.SMEM),
        any_spec,
        pl.BlockSpec((tile, 2 * deep), lambda i: (i, part)),
        *[any_spec] * len(arrays),
    ]
    operands = [row, factor, factor, *arrays]
    if given is not None:
        in_specs.append(sum_spec)
        operands.append(given)
    return pl.pallas_call(
        functools.partial(update_body, sources, own_a, own_b, given is not None),
        grid=(rows // tile,),
        out_shape=jax.ShapeDtypeStruct((rows, wide), jnp.float32),
        in_specs=in_specs,
        out_specs=sum_spec,
        input_output_aliases={} if given is None else {len(operands) - 1: 0},
        scratch_shapes=[
            pltpu.VMEM((wide, deep), jnp.float32),
            pltpu.VMEM((wide, deep), jnp.float32),
            pltpu.VMEM((wide, 2 * deep), jnp.bfloat16),
            pltpu.VMEM((wide, 2 * deep), jnp.bfloat16),
            pltpu.SemaphoreType.DMA((2,)),
        ],
        cost_estimate=pl.CostEstimate(
            flops=12 * rows * wide * deep,
            bytes_accessed=8 * rows * (deep + wide) + 8 * wide * deep,
            transcendentals=0,
        ),
    )(*operands)


def swapped(x, bit, count):
    return lax.ppermute(x, "col", [(i, i ^ bit) for i in range(count)])


def reduce_rows(x):
    count = lax.axis_size("col")
    index = lax.axis_index("col")
    x = x.reshape(count, x.shape[0] // count, x.shape[1])
    bit = 1
    while bit < count:
        pairs = x.reshape(x.shape[0] // 2, 2, *x.shape[1:])
        upper = (index & bit) != 0
        kept = jnp.where(upper, pairs[:, 1], pairs[:, 0])
        sent = jnp.where(upper, pairs[:, 0], pairs[:, 1])
        got = swapped(sent, bit, count)
        x = kept + got
        bit *= 2
    return x[0]


def gather_rows(x):
    count = lax.axis_size("col")
    index = lax.axis_index("col")
    x = x[None]
    bit = count // 2
    while bit >= 1:
        got = swapped(x, bit, count)
        upper = (index & bit) != 0
        x = jnp.stack([jnp.where(upper, got, x), jnp.where(upper, x, got)], axis=1)
        x = x.reshape(x.shape[0] * 2, *x.shape[2:])
        bit //= 2
    return x.reshape(x.shape[0] * x.shape[1], x.shape[2])


def ladder(rows):
    length = rows // 2
    along = [(0, 2 * (length - 1))]
    along += [(2 * z, 2 * (z - 1)) for z in range(length - 1, 1, -1)]
    along += [(2 * z + 1, 2 * z + 3) for z in range(length - 1)]
    along += [(2 * length - 1, 1)]
    across = [(0, 1)]
    across += [(2 * z + x, 2 * z + 1 - x) for z in range(1, length) for x in (0, 1)]
    return along, across


def on_device(features, factor):
    rows_dev, depth = factor.shape
    feature_count = features.shape[0]
    row_count = lax.axis_size("row")
    col_count = lax.axis_size("col")
    col_index = lax.axis_index("col")
    row_index = lax.axis_index("row")
    slab_rows = rows_dev // col_count
    share = B // col_count
    length = row_count // 2
    z, x = row_index // 2, row_index % 2
    is_source = row_index == 0
    along, across = ladder(row_count)
    chunks = HALVES * DEPTH_CHUNKS
    rounds = chunks + length
    wide, deep = B // HALVES, depth // DEPTH_CHUNKS // 2

    gram = times_rows(factor[:B], factor[:B])
    gram = gather_rows(reduce_rows(gram))
    first_points = features[:, :B].T
    identity = jnp.eye(B, dtype=jnp.float32)
    pivot = kernel(first_points, first_points) + ridge_value * identity - gram
    state = jnp.concatenate([pivot, identity], axis=1)
    for called in FACTOR_CALLS:
        state = factored(called, state)
    spare = jnp.pad(
        jnp.concatenate(
            [
                lax.dynamic_slice(state, (col_index * share, B), (share, B)),
                jnp.pad(
                    lax.dynamic_slice_in_dim(first_points, col_index * share, share, 0),
                    ((0, 0), (0, B - feature_count)),
                ),
            ]
        ),
        ((0, wide - 2 * share), (0, deep - B)),
    )

    def place(u, side):
        half, part = divmod(u, DEPTH_CHUNKS)
        at = (2 * part + side) * deep
        return slice(half * wide, (half + 1) * wide), slice(at, at + deep)

    def staged(t, factor):
        slot = t if t < INVERSE_SLOT else t - 1
        pair = [factor[place(min(t, chunks - 1), 0)]]
        pair.append(spare if t == INVERSE_SLOT else factor[place(slot, 1)])
        return lax.optimization_barrier(
            tuple(jnp.where(is_source, p, jnp.zeros_like(p)) for p in pair)
        )

    along_got, across_got = [], []
    relays_across = (x == 1) & ((z == 0) | (z == length - 1))

    def where_a(r, u):
        k, side = divmod(r, 2)
        if r == 1:
            return "across", u
        return ("along", u + k) if side else ("across", u + k + 1)

    def where_b(r, slot):
        k, side = divmod(r, 2)
        if r == 1:
            return "along", slot + 2
        return ("across", slot + length - k) if side else ("along", slot + length - 1 - k)

    def held(name):
        kind, t = name
        return along_got[t] if kind == "along" else across_got[t]

    sums = [None] * HALVES
    reduced_sums = [None] * HALVES
    row_number = jnp.full((1,), row_index, jnp.int32)

    def update(u, factor):
        half, part = divmod(u, DEPTH_CHUNKS)
        slot = u if u < INVERSE_SLOT else u + 1
        names = [(where_a(r, u), where_b(r, slot)) for r in range(1, row_count)]
        unique = sorted({name for pair in names for name in pair})
        sources = (None, *(tuple(unique.index(name) for name in pair) for pair in names))
        sums[half] = updated(
            row_number,
            factor,
            part,
            sources,
            [held(name) for name in unique],
            place(u, 0),
            place(u, 1),
            sums[half],
        )
        if part == DEPTH_CHUNKS - 1:
            reduced_sums[half] = reduce_rows(sums[half])

    staged_next = staged(0, factor)
    for t in range(rounds):
        if t == 0:
            send_across, send_along = staged_next
        else:
            send_along = jnp.where(relays_across, across_got[-1], along_got[-1])
            send_across = along_got[-1]
            if t <= chunks:
                send_along = jnp.where(is_source, staged_next[1], send_along)
            if t < chunks:
                send_across = jnp.where(is_source, staged_next[0], send_across)
        send_along, send_across, factor, along_got, across_got = lax.optimization_barrier(
            (send_along, send_across, factor, along_got, across_got)
        )
        if t < chunks:
            staged_next = staged(t + 1, factor)
        if t > length:
            update(t - length - 1, factor)
        if t < rounds - 1:
            along_got = [*along_got, lax.ppermute(send_along, "row", along)]
        across_got = [*across_got, lax.ppermute(send_across, "row", across)]

        slot = t - (length - 1)
        if slot == INVERSE_SLOT:
            got = spare
            for r in range(1, row_count):
                got = jnp.where(row_index == r, held(where_b(r, slot)), got)
            extra = jnp.concatenate(
                [got[:share, :B], got[share : 2 * share, : B // 2]], axis=1
            )
            everything = gather_rows(extra)
            inverse = everything[:, :B]
            panel_points = everything[:, B : B + feature_count]
            own_points = lax.dynamic_slice_in_dim(
                features, col_index * slab_rows, slab_rows, 1
            ).T
            global_rows = (
                row_index * rows_dev + col_index * slab_rows + lax.iota(jnp.int32, slab_rows)
            )
            diagonal = global_rows[:, None] == lax.iota(jnp.int32, B)[None, :]
            slab = kernel(own_points, panel_points) + ridge_value * diagonal.astype(jnp.float32)
    update(chunks - 1, factor)

    result = None
    for half in range(HALVES):
        columns = slice(half * wide, (half + 1) * wide)
        part = exact(slab[:, columns] - reduced_sums[half], inverse[:, columns], ((1,), (1,)))
        result = part if result is None else result + part
    return result


def solution(mesh):
    placed = (P(None, "row"), P("row", "col"))
    return jax.shard_map(
        on_device, mesh=mesh, in_specs=placed, out_specs=P(("row", "col"), None), check_vma=False
    )
```
